512 devices in a mesh: section: 32 (over x, y), gather: 16 (over z, core).
Axes of the slice: x: 4, y: 8, z: 8, core: 2. Of those that a mesh axis runs over, the one named last changes fastest.
Arguments:
- features: bfloat16 [131072, 512], P(('section', 'gather')), may hold values from -6 to 6
- neighbours: int32 [6, 131072], P(None, ('section', 'gather')), may hold values from 0 to 1279
- send_list: int32 [32, 16, 8, 1], P('section', 'gather'), may hold values from 0 to 1
- cluster: int32 [131072], P(('section', 'gather')), may hold values from 0 to 255, as said below
- coarse_neighbours: int32 [6, 8192], P(None, 'section'), may hold values from 0 to 767
- fine_dst: bfloat16 [512, 512], replicated, may hold values from -0.25 to 0.25
- fine_src: bfloat16 [512, 512], replicated, may hold values from -0.25 to 0.25
- fine_edge: bfloat16 [512, 512], replicated, may hold values from -0.25 to 0.25
- fine_node: bfloat16 [512, 512], replicated, may hold values from -0.25 to 0.25
- fine_bias: float32 [2, 512], replicated, may hold values from -3 to 3
- fine_gain: float32 [512], replicated, may hold values from 0.1 to 1.9
- coarse_dst: bfloat16 [512, 512], replicated, may hold values from -0.25 to 0.25
- coarse_src: bfloat16 [512, 512], replicated, may hold values from -0.25 to 0.25
- coarse_edge: bfloat16 [512, 512], replicated, may hold values from -0.25 to 0.25
- coarse_node: bfloat16 [512, 512], replicated, may hold values from -0.25 to 0.25
- coarse_bias: float32 [2, 512], replicated, may hold values from -3 to 3
- coarse_gain: float32 [512], replicated, may hold values from 0.1 to 1.9
Outputs:
- mesh_out: bfloat16 [131072, 512], P(('section', 'gather'))
The draws below stay inside these ranges and needn't reach their ends.
Inputs may be any that keep to these rules, and one draw needn't show every extreme that they name: `cluster`: within the 4096 rows of each section group, every coarse node number names exactly 16 rows.
All inputs are finite; a program needn't handle non-finite values.
Results may differ from the reference program's by a relative error of at most 0.0065.
Values may be sent and summed in bfloat16 or wider, within the bound.
No kernel may reach another device: no remote copies, remote signals or barrier semaphores. Data moves between devices by JAX's collectives and lax.ppermute only.
A program may use at most 64 MiB of HBM per device.

```python
import jax
import jax.numpy as jnp
from jax import lax

WIDTH = 512
PATCH = 128
PATCH_DEV = 2
GHOST = 1
EDGES = 6
POOL = 16
ROWS = 256
EXT = 1280
NODES = 131072
CLUSTERS = 256
COARSE = 8192
N_SECTION = 32
N_GATHER = 16


def draw_cluster(key, part):
    group_size = N_GATHER * PATCH_DEV * PATCH
    key_list = jax.random.split(jax.random.fold_in(key, 17), N_SECTION)
    orders = jax.vmap(lambda subkey: jax.random.permutation(subkey, group_size))(key_list)
    return (orders // POOL).astype(jnp.int32).reshape(-1)


def plant(values, stream_key, low, top_value):
    dims = values.shape
    place = [jax.random.randint(jax.random.fold_in(stream_key, axis), (), 0, dims[axis]) for axis in range(len(dims))]
    values = values.at[tuple(place)].set(low)
    longest = dims.index(max(dims))
    place[longest] = (place[longest] + 1) % dims[longest]
    return values.at[tuple(place)].set(top_value)


def block_scale(stream_key, dims, shards, low, top_value):
    def one(axis_at, blocks):
        draws = jax.random.uniform(jax.random.fold_in(jax.random.fold_in(stream_key, 6), axis_at), (blocks,), jnp.float32, low / len(shards), top_value / len(shards))
        return jnp.repeat(jnp.exp(draws), dims[axis_at] // blocks).reshape((-1,) + (1,) * (len(dims) - axis_at - 1))

    loudness = one(*shards[0])
    for cut in shards[1:]:
        loudness = loudness * one(*cut)
    return loudness


def scatter_about(key, dims, width, limit, cuts=(), kind=jnp.bfloat16):
    loudness = block_scale(key, dims, cuts, -0.22, 0.18) if cuts else 1.0
    array = jax.random.normal(key, dims, jnp.float32) * width * loudness
    return jnp.minimum(jnp.maximum(array, -limit), limit).astype(kind)


def setup_inputs(seed: int = 0) -> dict:
    seeds = jax.random.split(jax.random.key(seed), 18)
    features = scatter_about(seeds[0], (NODES, WIDTH), 1.0, 6.0, ((0, 512),))
    neighbours = plant(jax.random.randint(seeds[1], (EDGES, NODES), 0, EXT), jax.random.fold_in(seeds[1], 1), 0, EXT - 1).astype(jnp.int32)
    send_list = plant(jax.random.randint(seeds[2], (N_SECTION, N_GATHER, 8, GHOST), 0, PATCH_DEV), jax.random.fold_in(seeds[2], 1), 0, PATCH_DEV - 1).astype(jnp.int32)
    cluster = draw_cluster(jax.random.fold_in(seeds[17], 71), 0)
    coarse_neighbours = plant(jax.random.randint(seeds[4], (EDGES, COARSE), 0, 3 * CLUSTERS), jax.random.fold_in(seeds[4], 1), 0, (3 * CLUSTERS) - 1).astype(jnp.int32)
    fine_dst = scatter_about(seeds[5], (WIDTH, WIDTH), WIDTH ** -0.5, 0.25)
    fine_src = scatter_about(seeds[6], (WIDTH, WIDTH), WIDTH ** -0.5, 0.25)
    fine_edge = scatter_about(seeds[7], (WIDTH, WIDTH), WIDTH ** -0.5, 0.25)
    fine_node = scatter_about(seeds[8], (WIDTH, WIDTH), WIDTH ** -0.5, 0.25)
    fine_bias = scatter_about(seeds[9], (2, WIDTH), 0.5, 3.0, (), jnp.float32)
    fine_gain = jnp.clip(1.0 + 0.18 * jax.random.normal(seeds[10], (WIDTH,), jnp.float32), 0.1, 1.9)
    coarse_dst = scatter_about(seeds[11], (WIDTH, WIDTH), WIDTH ** -0.5, 0.25)
    coarse_src = scatter_about(seeds[12], (WIDTH, WIDTH), WIDTH ** -0.5, 0.25)
    coarse_edge = scatter_about(seeds[13], (WIDTH, WIDTH), WIDTH ** -0.5, 0.25)
    coarse_node = scatter_about(seeds[14], (WIDTH, WIDTH), WIDTH ** -0.5, 0.25)
    coarse_bias = scatter_about(seeds[15], (2, WIDTH), 0.5, 3.0, (), jnp.float32)
    coarse_gain = jnp.clip(1.0 + 0.18 * jax.random.normal(seeds[16], (WIDTH,), jnp.float32), 0.1, 1.9)
    return dict(features=features, neighbours=neighbours, send_list=send_list, cluster=cluster, coarse_neighbours=coarse_neighbours, fine_dst=fine_dst, fine_src=fine_src, fine_edge=fine_edge, fine_node=fine_node, fine_bias=fine_bias, fine_gain=fine_gain, coarse_dst=coarse_dst, coarse_src=coarse_src, coarse_edge=coarse_edge, coarse_node=coarse_node, coarse_bias=coarse_bias, coarse_gain=coarse_gain)


DIRECTIONS = ((-1, -1), (-1, 0), (-1, 1), (0, -1), (0, 1), (1, -1), (1, 0), (1, 1))
EPSILON = 1e-05

def normalise(values):
    middle = lax.optimization_barrier(jnp.mean(values, axis=-1, keepdims=True))
    centred = values - middle
    spread = lax.optimization_barrier(jnp.mean(centred * centred, axis=-1, keepdims=True))
    return centred * lax.rsqrt(spread + EPSILON)

def project(inputs, weight):
    return jnp.dot(inputs, weight, preferred_element_type=jnp.float32).astype(jnp.bfloat16)

def message_update(centre, sources, neighbour_ids, w_target, w_edge, w_node, offsets, gain_row):
    target_term = jnp.dot(centre, w_target, preferred_element_type=jnp.float32) + offsets[0]
    edge_count = neighbour_ids.shape[0]
    picked = jnp.take(sources, neighbour_ids.reshape(-1), axis=0).reshape(edge_count, centre.shape[0], sources.shape[1])
    hidden = jax.nn.silu(target_term[None] + picked.astype(jnp.float32)).astype(jnp.bfloat16)
    signals = jax.nn.silu(jnp.dot(hidden.reshape(-1, hidden.shape[2]), w_edge, preferred_element_type=jnp.float32) + offsets[1])
    summed = lax.optimization_barrier(jnp.sum(signals.reshape(hidden.shape), axis=0)).astype(jnp.bfloat16)
    return gain_row * normalise(jnp.dot(summed, w_node, preferred_element_type=jnp.float32))

def reference(features, neighbours, send_list, cluster, coarse_neighbours, fine_dst, fine_src, fine_edge, fine_node, fine_bias, fine_gain, coarse_dst, coarse_src, coarse_edge, coarse_node, coarse_bias, coarse_gain):
    section_ids = jnp.arange(N_SECTION, dtype=jnp.int32)[:, None]
    gather_ids = jnp.arange(N_GATHER, dtype=jnp.int32)[None, :]
    device_ids = section_ids * N_GATHER + gather_ids
    inside = jnp.arange(PATCH, dtype=jnp.int32)
    own_rows = device_ids[:, :, None] * ROWS + jnp.arange(ROWS, dtype=jnp.int32)
    pieces = [own_rows.astype(jnp.int32)]
    for number in range(8):
        shift_section, shift_gather = DIRECTIONS[number]
        sender_section = (section_ids - shift_section) % N_SECTION
        sender_gather = (gather_ids - shift_gather) % N_GATHER
        sender = sender_section * N_GATHER + sender_gather
        listed = send_list[sender_section, sender_gather, number]
        ghost_rows = sender[:, :, None, None] * ROWS + listed[:, :, :, None] * PATCH + inside
        pieces.append(ghost_rows.reshape(N_SECTION, N_GATHER, GHOST * PATCH).astype(jnp.int32))
    ext_rows = jnp.concatenate(pieces, axis=2)
    local_ids = neighbours.reshape(EDGES, N_SECTION, N_GATHER, ROWS)
    widened = jnp.broadcast_to(ext_rows[None], (EDGES, N_SECTION, N_GATHER, EXT))
    global_ids = jnp.take_along_axis(widened, local_ids, axis=3)
    group_size = N_GATHER * ROWS
    global_ids = jnp.transpose(global_ids.reshape(EDGES, N_SECTION, group_size), (1, 0, 2))
    sources = project(features, fine_src)
    blocks = features.reshape(N_SECTION, group_size, WIDTH)

    def fine_block(couple):
        centre, block_ids = couple
        update = message_update(centre, sources, block_ids, fine_dst, fine_edge, fine_node, fine_bias, fine_gain)
        return (centre.astype(jnp.float32) + update).astype(jnp.bfloat16)
    fine_rows = lax.map(fine_block, (blocks, global_ids)).reshape(NODES, WIDTH)
    member = jnp.arange(NODES, dtype=jnp.int32) // group_size * CLUSTERS + cluster
    pooled_sum = jax.ops.segment_sum(fine_rows.astype(jnp.float32), member, num_segments=COARSE)
    pooled = (pooled_sum / POOL).astype(jnp.bfloat16)
    coarse_sources = project(pooled, coarse_src)
    coarse_section = jnp.arange(COARSE, dtype=jnp.int32) // CLUSTERS
    source_section = (coarse_section[None, :] - 1 + coarse_neighbours // CLUSTERS) % N_SECTION
    coarse_ids = source_section * CLUSTERS + coarse_neighbours % CLUSTERS
    coarse_update = message_update(pooled, coarse_sources, coarse_ids, coarse_dst, coarse_edge, coarse_node, coarse_bias, coarse_gain).astype(jnp.bfloat16)
    lifted = jnp.take(coarse_update, member, axis=0)
    return (fine_rows.astype(jnp.float32) + lifted.astype(jnp.float32)).astype(jnp.bfloat16)
```

```python
import jax
import jax.numpy as jnp
from jax import lax
from jax.experimental import pallas as pl
from jax.experimental.pallas import tpu as pltpu
from jax.sharding import PartitionSpec as P

PATCH = 128
POOL = 16
META = 16
EPSILON = 1e-05
F32 = jnp.float32
BF16 = jnp.bfloat16


def shifted(block, axis, step):
    count = lax.axis_size(axis)
    return lax.ppermute(block, axis, [(i, (i + step) % count) for i in range(count)])


def dot(left, right):
    return jnp.dot(left, right, preferred_element_type=F32)


def one_hot(column, width, value):
    lanes = lax.broadcasted_iota(jnp.int32, (column.shape[0], width), 1)
    return jnp.where(column == lanes, F32(value), F32(0)).astype(BF16)


def silu_of_half(half):
    return half * jnp.tanh(half) + half


def normalise(values):
    middle = jnp.mean(values, axis=-1, keepdims=True)
    centred = values - middle
    spread = jnp.mean(centred * centred, axis=-1, keepdims=True)
    return centred * lax.rsqrt(spread + EPSILON)


def messages(ids, sources, target_half, edge, node, bias_half, gain):
    half_edge = edge * BF16(0.5)
    total = None
    for e in range(6):
        chosen = one_hot(ids[:, e : e + 1], sources.shape[0], 0.5)
        hidden = silu_of_half(dot(chosen, sources) + target_half).astype(BF16)
        signal = silu_of_half(dot(hidden, half_edge) + bias_half)
        total = signal if total is None else total + signal
    return gain * normalise(dot(total.astype(BF16), node))


def fine_kernel(
    features, own_sources, target_half, beside, below, above, ids, cluster, src, edge, node, bias, gain,
    rows_out, partial_out, sources,
):
    rows = features.shape[0]

    def place(number, value):
        sources[pl.ds(rows + PATCH * number, PATCH), :] = value

    sources[pl.ds(0, rows), :] = own_sources[...]
    near = dot(beside[...], src[...]).astype(BF16)
    place(1, near[:PATCH])
    place(6, near[PATCH:])
    for piece, numbers in ((above, (0, 3, 5)), (below, (2, 4, 7))):
        projected = dot(piece[...], src[...]).astype(BF16)
        for k, number in enumerate(numbers):
            place(number, projected[k * PATCH : (k + 1) * PATCH])
    update = messages(
        ids[...], sources[...], target_half[...], edge[...], node[...], 0.5 * bias[1:2, :], gain[...]
    )
    fine_rows = (features[...].astype(F32) + update).astype(BF16)
    rows_out[...] = fine_rows
    clusters = partial_out.shape[0]
    member = lax.broadcasted_iota(jnp.int32, (clusters, rows), 0) == cluster[...]
    member = jnp.where(member, F32(1), F32(0)).astype(BF16)
    partial_out[...] = dot(member, fine_rows).astype(BF16)


def coarse_kernel(spread, fine_rows, ids, cluster, dst, src, edge, node, bias, gain, out, pooled):
    shares = spread.shape[0] // 48
    for k in range(shares):
        pooled[pl.ds(16 * k, 16), :] = spread[pl.ds(48 * k + 16, 16), :]
    clusters = pooled.shape[0]
    sources = dot(spread[...], src[...]).astype(BF16)
    target_half = 0.5 * (dot(pooled[...], dst[...]) + bias[0:1, :])
    place = ids[...]
    within = place & (clusters - 1)
    place = (within >> 4) * 48 + (place >> 8) * 16 + (within & 15)
    update = messages(
        place, sources, target_half, edge[...], node[...], 0.5 * bias[1:2, :], gain[...]
    ).astype(BF16)
    lifted = dot(one_hot(cluster[...], clusters, 1.0), update)
    out[...] = (fine_rows[...].astype(F32) + lifted).astype(BF16)


def body(
    features,
    neighbours,
    send_list,
    cluster,
    coarse_neighbours,
    fine_dst,
    fine_src,
    fine_edge,
    fine_node,
    fine_bias,
    fine_gain,
    coarse_dst,
    coarse_src,
    coarse_edge,
    coarse_node,
    coarse_bias,
    coarse_gain,
):
    rows, width = features.shape
    shares = lax.axis_size("gather")
    clusters = shares * rows // POOL
    share = clusters // shares
    listing = jnp.broadcast_to(send_list.reshape(8, 1).astype(BF16), (8, width))
    own = jnp.concatenate([features, listing, jnp.zeros((META - 8, width), BF16)], axis=0)
    before = shifted(own, "section", 1)
    after = shifted(own, "section", -1)

    def chosen(block, number):
        return jnp.where(block[rows + number][None, :] > 0.5, block[PATCH:rows], block[:PATCH])

    own_sources = dot(features, fine_src).astype(BF16)
    target_half = 0.5 * (dot(features, fine_dst) + fine_bias[0])
    ids = jnp.pad(neighbours.T, ((0, 0), (0, 2)))
    coarse_ids = jnp.pad(coarse_neighbours.T, ((0, 0), (0, 2)))
    to_next = jnp.concatenate([chosen(after, 2), chosen(own, 4), chosen(before, 7)], axis=0)
    to_last = jnp.concatenate([chosen(after, 0), chosen(own, 3), chosen(before, 5)], axis=0)
    below = shifted(to_next, "gather", 1)
    above = shifted(to_last, "gather", -1)
    beside = jnp.concatenate([chosen(after, 1), chosen(before, 6)], axis=0)

    fine_rows, partial = pl.pallas_call(
        fine_kernel,
        out_shape=(
            jax.ShapeDtypeStruct((rows, width), BF16),
            jax.ShapeDtypeStruct((clusters, width), BF16),
        ),
        scratch_shapes=[pltpu.VMEM((rows + 8 * PATCH, width), BF16)],
        name="fine",
    )(
        features, own_sources, target_half, beside, below, above, ids, cluster[None, :],
        fine_src, fine_edge, fine_node, fine_bias, fine_gain[None, :],
    )

    parts = lax.all_to_all(partial.reshape(shares, share, width), "gather", 0, 0, tiled=True)
    pooled = (jnp.sum(parts.astype(F32), axis=0) / POOL).astype(BF16)
    sides = [shifted(pooled, "section", 1), pooled, shifted(pooled, "section", -1)]
    spread = lax.all_gather(jnp.concatenate(sides, axis=0), "gather", axis=0, tiled=True)

    return pl.pallas_call(
        coarse_kernel,
        out_shape=jax.ShapeDtypeStruct((rows, width), BF16),
        scratch_shapes=[pltpu.VMEM((clusters, width), BF16)],
        name="coarse",
    )(
        spread, fine_rows, coarse_ids, cluster[:, None],
        coarse_dst, coarse_src, coarse_edge, coarse_node, coarse_bias, coarse_gain[None, :],
    )


def solution(mesh):
    placed = (
        P(("section", "gather"), None),
        P(None, ("section", "gather")),
        P("section", "gather", None, None),
        P(("section", "gather")),
        P(None, "section"),
    ) + (P(),) * 12
    return jax.shard_map(
        body, mesh=mesh, in_specs=placed, out_specs=P(("section", "gather"), None), check_vma=False
    )
```

```python
import jax
import jax.numpy as jnp
from jax import lax
from jax.experimental import pallas as pl
from jax.experimental.pallas import tpu as pltpu
from jax.sharding import PartitionSpec as P

PATCH = 128
POOL = 16
META = 16
GROUP = 2
EPSILON = 1e-05
F32 = jnp.float32
BF16 = jnp.bfloat16


def shifted(block, axis, step):
    count = lax.axis_size(axis)
    return lax.ppermute(block, axis, [(i, (i + step) % count) for i in range(count)])


def near(*arrays):
    return [pltpu.with_memory_space_constraint(a, pltpu.VMEM) for a in arrays]


def dot(left, right):
    return jnp.dot(left, right, preferred_element_type=F32)


def one_hot(column, width, value):
    lanes = lax.broadcasted_iota(jnp.int32, (column.shape[0], width), 1)
    return jnp.where(column == lanes, F32(value), F32(0)).astype(BF16)


def columns(index_rows):
    return index_rows.astype(F32).T.astype(jnp.int32)


def silu_of_half(half):
    return half * jnp.tanh(half) + half


def normalise(values):
    middle = jnp.mean(values, axis=-1, keepdims=True)
    centred = values - middle
    spread = jnp.mean(centred * centred, axis=-1, keepdims=True)
    return centred * lax.rsqrt(spread + EPSILON)


def messages(ids, sources, target_half, edge, node, bias_half, gain):
    half_edge = edge * BF16(0.5)
    rows = ids.shape[0]
    total = None
    for e in range(0, 6, GROUP):
        chosen = jnp.concatenate(
            [one_hot(ids[:, k : k + 1], sources.shape[0], 0.5) for k in range(e, e + GROUP)], axis=0
        )
        picked = dot(chosen, sources)
        hidden = jnp.concatenate(
            [
                silu_of_half(picked[k * rows : (k + 1) * rows] + target_half).astype(BF16)
                for k in range(GROUP)
            ],
            axis=0,
        )
        signals = silu_of_half(dot(hidden, half_edge) + bias_half)
        for k in range(GROUP):
            signal = signals[k * rows : (k + 1) * rows]
            total = signal if total is None else total + signal
    return gain * normalise(dot(total.astype(BF16), node))


def listed_kernel(features, listing, out):
    rows, width = features.shape
    out[pl.ds(0, rows), :] = features[...]
    lists = columns(jnp.broadcast_to(listing[...], (8, listing.shape[1])))[:, :1]
    lists = jnp.broadcast_to(lists.astype(F32), (8, width))
    out[pl.ds(rows, META), :] = jnp.concatenate([lists, jnp.zeros_like(lists)], axis=0).astype(BF16)


def fine_kernel(
    features, own_sources, target_half, beside, below, above, ids, cluster, src, edge, node, bias, gain,
    rows_out, partial_out, sources,
):
    rows = features.shape[0]

    def place(number, value):
        sources[pl.ds(rows + PATCH * number, PATCH), :] = value

    sources[pl.ds(0, rows), :] = own_sources[...]
    near = dot(beside[...], src[...]).astype(BF16)
    place(1, near[:PATCH])
    place(6, near[PATCH:])
    for piece, numbers in ((above, (0, 3, 5)), (below, (2, 4, 7))):
        projected = dot(piece[...], src[...]).astype(BF16)
        for k, number in enumerate(numbers):
            place(number, projected[k * PATCH : (k + 1) * PATCH])
    update = messages(
        columns(ids[...]), sources[...], target_half[...], edge[...], node[...], 0.5 * bias[1:2, :], gain[...]
    )
    fine_rows = (features[...].astype(F32) + update).astype(BF16)
    rows_out[...] = fine_rows
    clusters = partial_out.shape[0]
    member = lax.broadcasted_iota(jnp.int32, (clusters, rows), 0) == cluster[...]
    member = jnp.where(member, F32(1), F32(0)).astype(BF16)
    partial_out[...] = dot(member, fine_rows).astype(BF16)


def coarse_kernel(spread, fine_rows, ids, cluster, dst, src, edge, node, bias, gain, out, pooled):
    shares = spread.shape[0] // 48
    for k in range(shares):
        pooled[pl.ds(16 * k, 16), :] = spread[pl.ds(48 * k + 16, 16), :]
    clusters = pooled.shape[0]
    sources = dot(spread[...], src[...]).astype(BF16)
    target_half = 0.5 * (dot(pooled[...], dst[...]) + bias[0:1, :])
    place = columns(ids[...])
    within = place & (clusters - 1)
    place = (within >> 4) * 48 + (place >> 8) * 16 + (within & 15)
    update = messages(
        place, sources, target_half, edge[...], node[...], 0.5 * bias[1:2, :], gain[...]
    ).astype(BF16)
    owner = columns(jnp.broadcast_to(cluster[...], (8, cluster.shape[1])))[:, :1]
    lifted = dot(one_hot(owner, clusters, 1.0), update)
    out[...] = (fine_rows[...].astype(F32) + lifted).astype(BF16)


def body(
    features,
    neighbours,
    send_list,
    cluster,
    coarse_neighbours,
    fine_dst,
    fine_src,
    fine_edge,
    fine_node,
    fine_bias,
    fine_gain,
    coarse_dst,
    coarse_src,
    coarse_edge,
    coarse_node,
    coarse_bias,
    coarse_gain,
):
    rows, width = features.shape
    shares = lax.axis_size("gather")
    clusters = shares * rows // POOL
    share = clusters // shares
    own = pl.pallas_call(
        listed_kernel,
        out_shape=pltpu.VMEM((rows + META, width), BF16),
        compiler_params=pltpu.CompilerParams(vmem_limit_bytes=8 << 20),
        name="listed",
    )(features, send_list.reshape(1, 8))
    before = shifted(own, "section", 1)
    after = shifted(own, "section", -1)

    def chosen(block, number):
        return jnp.where(block[rows + number][None, :] > 0.5, block[PATCH:rows], block[:PATCH])

    own_sources = dot(features, fine_src).astype(BF16)
    target_half = 0.5 * (dot(features, fine_dst) + fine_bias[0])
    to_next = jnp.concatenate([chosen(after, 2), chosen(own, 4), chosen(before, 7)], axis=0)
    to_last = jnp.concatenate([chosen(after, 0), chosen(own, 3), chosen(before, 5)], axis=0)
    below = shifted(to_next, "gather", 1)
    above = shifted(to_last, "gather", -1)
    beside = jnp.concatenate([chosen(after, 1), chosen(before, 6)], axis=0)

    fine_rows, partial = pl.pallas_call(
        fine_kernel,
        out_shape=(
            pltpu.VMEM((rows, width), BF16),
            pltpu.VMEM((clusters, width), BF16),
        ),
        scratch_shapes=[pltpu.VMEM((rows + 8 * PATCH, width), BF16)],
        compiler_params=pltpu.CompilerParams(vmem_limit_bytes=24 << 20),
        name="fine",
    )(*near(
        features, own_sources, target_half, beside, below, above, neighbours, cluster[None, :],
        fine_src, fine_edge, fine_node, fine_bias, fine_gain[None, :],
    ))

    parts = lax.all_to_all(partial.reshape(shares, share, width), "gather", 0, 0, tiled=True)
    pooled = (jnp.sum(parts.astype(F32), axis=0) / POOL).astype(BF16)
    sides = [shifted(pooled, "section", 1), pooled, shifted(pooled, "section", -1)]
    spread = lax.all_gather(jnp.concatenate(sides, axis=0), "gather", axis=0, tiled=True)

    return pl.pallas_call(
        coarse_kernel,
        out_shape=jax.ShapeDtypeStruct((rows, width), BF16),
        scratch_shapes=[pltpu.VMEM((clusters, width), BF16)],
        compiler_params=pltpu.CompilerParams(vmem_limit_bytes=24 << 20),
        name="coarse",
    )(*near(
        spread, fine_rows, coarse_neighbours, cluster[None, :],
        coarse_dst, coarse_src, coarse_edge, coarse_node, coarse_bias, coarse_gain[None, :],
    ))


def solution(mesh):
    placed = (
        P(("section", "gather"), None),
        P(None, ("section", "gather")),
        P("section", "gather", None, None),
        P(("section", "gather")),
        P(None, "section"),
    ) + (P(),) * 12
    return jax.shard_map(
        body, mesh=mesh, in_specs=placed, out_specs=P(("section", "gather"), None), check_vma=False
    )
```

```python
import jax
import jax.numpy as jnp
from jax import lax
from jax.experimental import pallas as pl
from jax.experimental.pallas import tpu as pltpu
from jax.sharding import PartitionSpec as P

PATCH = 128
POOL = 16
META = 16
GROUP = 2
EPSILON = 1e-05
F32 = jnp.float32
BF16 = jnp.bfloat16


def shifted(block, axis, step):
    count = lax.axis_size(axis)
    return lax.ppermute(block, axis, [(i, (i + step) % count) for i in range(count)])


def alternating(block):
    sections, shares = lax.axis_size("section"), lax.axis_size("gather")
    return lax.ppermute(
        block,
        ("section", "gather"),
        [
            (s * shares + g, (s + 1 - 2 * (g % 2)) % sections * shares + g)
            for s in range(sections)
            for g in range(shares)
        ],
    )


def near(*arrays):
    return [pltpu.with_memory_space_constraint(a, pltpu.VMEM) for a in arrays]


def dot(left, right):
    return jnp.dot(left, right, preferred_element_type=F32)


def one_hot(column, width, value):
    lanes = lax.broadcasted_iota(jnp.int32, (column.shape[0], width), 1)
    return jnp.where(column == lanes, F32(value), F32(0)).astype(BF16)


def columns(index_rows):
    return index_rows.astype(F32).T.astype(jnp.int32)


def silu_of_half(half):
    return half * jnp.tanh(half) + half


def normalise(values):
    middle = jnp.mean(values, axis=-1, keepdims=True)
    centred = values - middle
    spread = jnp.mean(centred * centred, axis=-1, keepdims=True)
    return centred * lax.rsqrt(spread + EPSILON)


def messages(ids, sources, target_half, edge, node, bias_half, gain):
    half_edge = edge * BF16(0.5)
    rows = ids.shape[0]
    total = None
    for e in range(0, 6, GROUP):
        chosen = jnp.concatenate(
            [one_hot(ids[:, k : k + 1], sources.shape[0], 0.5) for k in range(e, e + GROUP)], axis=0
        )
        picked = dot(chosen, sources)
        hidden = jnp.concatenate(
            [
                silu_of_half(picked[k * rows : (k + 1) * rows] + target_half).astype(BF16)
                for k in range(GROUP)
            ],
            axis=0,
        )
        signals = silu_of_half(dot(hidden, half_edge) + bias_half)
        for k in range(GROUP):
            signal = signals[k * rows : (k + 1) * rows]
            total = signal if total is None else total + signal
    return gain * normalise(dot(total.astype(BF16), node))


def listed_kernel(features, listing, out):
    rows, width = features.shape
    out[pl.ds(0, rows), :] = features[...]
    lists = columns(jnp.broadcast_to(listing[...], (8, listing.shape[1])))[:, :1]
    lists = jnp.broadcast_to(lists.astype(F32), (8, width))
    out[pl.ds(rows, META), :] = jnp.concatenate([lists, jnp.zeros_like(lists)], axis=0).astype(BF16)


def fine_kernel(
    features, own_sources, target_half, beside, below, above, ids, cluster, src, edge, node, bias, gain,
    rows_out, partial_out, sources,
):
    rows = features.shape[0]

    def place(number, value):
        sources[pl.ds(rows + PATCH * number, PATCH), :] = value

    sources[pl.ds(0, rows), :] = own_sources[...]
    near = dot(beside[...], src[...]).astype(BF16)
    place(1, near[:PATCH])
    place(6, near[PATCH:])
    for piece, numbers in ((above, (0, 3, 5)), (below, (2, 4, 7))):
        projected = dot(piece[...], src[...]).astype(BF16)
        for k, number in enumerate(numbers):
            place(number, projected[k * PATCH : (k + 1) * PATCH])
    update = messages(
        columns(ids[...]), sources[...], target_half[...], edge[...], node[...], 0.5 * bias[1:2, :], gain[...]
    )
    fine_rows = (features[...].astype(F32) + update).astype(BF16)
    rows_out[...] = fine_rows
    clusters = partial_out.shape[0]
    member = lax.broadcasted_iota(jnp.int32, (clusters, rows), 0) == cluster[...]
    member = jnp.where(member, F32(1), F32(0)).astype(BF16)
    partial_out[...] = dot(member, fine_rows).astype(BF16)


def coarse_kernel(spread, fine_rows, ids, cluster, dst, src, edge, node, bias, gain, out, pooled):
    shares = spread.shape[0] // 48
    for k in range(shares):
        pooled[pl.ds(16 * k, 16), :] = spread[pl.ds(48 * k, 16), :]
    clusters = pooled.shape[0]
    sources = dot(spread[...], src[...]).astype(BF16)
    target_half = 0.5 * (dot(pooled[...], dst[...]) + bias[0:1, :])
    place = columns(ids[...])
    within = place & (clusters - 1)
    section = place >> 8
    own = (within >> 4) * 48 + (within & 15)
    side = (within >> 5) * 96 + (within & 31) + 16
    place = jnp.where(section == 1, own, side + (section >> 1) * 48)
    update = messages(
        place, sources, target_half, edge[...], node[...], 0.5 * bias[1:2, :], gain[...]
    ).astype(BF16)
    owner = columns(jnp.broadcast_to(cluster[...], (8, cluster.shape[1])))[:, :1]
    lifted = dot(one_hot(owner, clusters, 1.0), update)
    out[...] = (fine_rows[...].astype(F32) + lifted).astype(BF16)


def body(
    features,
    neighbours,
    send_list,
    cluster,
    coarse_neighbours,
    fine_dst,
    fine_src,
    fine_edge,
    fine_node,
    fine_bias,
    fine_gain,
    coarse_dst,
    coarse_src,
    coarse_edge,
    coarse_node,
    coarse_bias,
    coarse_gain,
):
    rows, width = features.shape
    shares = lax.axis_size("gather")
    clusters = shares * rows // POOL
    share = clusters // shares
    own = pl.pallas_call(
        listed_kernel,
        out_shape=pltpu.VMEM((rows + META, width), BF16),
        compiler_params=pltpu.CompilerParams(vmem_limit_bytes=8 << 20),
        name="listed",
    )(*(pltpu.with_memory_space_constraint(a, pltpu.HBM) for a in (features, send_list.reshape(1, 8))))
    before = shifted(own, "section", 1)
    after = shifted(own, "section", -1)

    def chosen(block, number):
        return jnp.where(block[rows + number][None, :] > 0.5, block[PATCH:rows], block[:PATCH])

    own_sources = dot(features, fine_src).astype(BF16)
    target_half = 0.5 * (dot(features, fine_dst) + fine_bias[0])
    to_next = jnp.concatenate([chosen(after, 2), chosen(own, 4), chosen(before, 7)], axis=0)
    to_last = jnp.concatenate([chosen(after, 0), chosen(own, 3), chosen(before, 5)], axis=0)
    below = shifted(to_next, "gather", 1)
    above = shifted(to_last, "gather", -1)
    beside = jnp.concatenate([chosen(after, 1), chosen(before, 6)], axis=0)

    fine_rows, partial = pl.pallas_call(
        fine_kernel,
        out_shape=(
            pltpu.VMEM((rows, width), BF16),
            pltpu.VMEM((clusters, width), BF16),
        ),
        scratch_shapes=[pltpu.VMEM((rows + 8 * PATCH, width), BF16)],
        compiler_params=pltpu.CompilerParams(vmem_limit_bytes=24 << 20),
        name="fine",
    )(*near(
        features, own_sources, target_half, beside, below, above, neighbours, cluster[None, :],
        fine_src, fine_edge, fine_node, fine_bias, fine_gain[None, :],
    ))

    parts = lax.all_to_all(partial.reshape(shares, share, width), "gather", 0, 0, tiled=True)
    pooled = (jnp.sum(parts.astype(F32), axis=0) / POOL).astype(BF16)
    pairs = [[2 * k, 2 * k + 1] for k in range(shares // 2)]
    chip = lax.all_gather(pooled, "gather", axis=0, tiled=True, axis_index_groups=pairs)
    side = alternating(chip)
    spread = lax.all_gather(jnp.concatenate([pooled, side], axis=0), "gather", axis=0, tiled=True)

    return pl.pallas_call(
        coarse_kernel,
        out_shape=jax.ShapeDtypeStruct((rows, width), BF16),
        scratch_shapes=[pltpu.VMEM((clusters, width), BF16)],
        compiler_params=pltpu.CompilerParams(vmem_limit_bytes=24 << 20),
        name="coarse",
    )(*near(
        spread, fine_rows, coarse_neighbours, cluster[None, :],
        coarse_dst, coarse_src, coarse_edge, coarse_node, coarse_bias, coarse_gain[None, :],
    ))


def solution(mesh):
    placed = (
        P(("section", "gather"), None),
        P(None, ("section", "gather")),
        P("section", "gather", None, None),
        P(("section", "gather")),
        P(None, "section"),
    ) + (P(),) * 12
    return jax.shard_map(
        body, mesh=mesh, in_specs=placed, out_specs=P(("section", "gather"), None), check_vma=False
    )
```

```python
import jax
import jax.numpy as jnp
from jax import lax
from jax.experimental import pallas as pl
from jax.experimental.pallas import tpu as pltpu
from jax.sharding import PartitionSpec as P


PATCH = 128
POOL = 16
META = 16
GROUP = 2
EPSILON = 1e-05
F32 = jnp.float32
BF16 = jnp.bfloat16


def shifted(block, axis, step):
    count = lax.axis_size(axis)
    return lax.ppermute(block, axis, [(i, (i + step) % count) for i in range(count)])


def alternating(block):
    sections, shares = lax.axis_size("section"), lax.axis_size("gather")
    return lax.ppermute(
        block,
        ("section", "gather"),
        [
            (s * shares + g, (s + 1 - 2 * (g % 2)) % sections * shares + g)
            for s in range(sections)
            for g in range(shares)
        ],
    )


def across_chip(block):
    pairs = [[g, g + 1] for g in range(0, lax.axis_size("gather"), 2)]
    return lax.all_gather(block, "gather", axis=0, tiled=True, axis_index_groups=pairs)


def near(*arrays):
    return [pltpu.with_memory_space_constraint(a, pltpu.VMEM) for a in arrays]


def far(*arrays):
    return [pltpu.with_memory_space_constraint(a, pltpu.HBM) for a in arrays]


def dot(left, right):
    return jnp.dot(left, right, preferred_element_type=F32)


def one_hot(column, width, value):
    lanes = lax.broadcasted_iota(jnp.int32, (column.shape[0], width), 1)
    return jnp.where(column == lanes, F32(value), F32(0)).astype(BF16)


def columns(index_rows):
    return index_rows.astype(F32).T.astype(jnp.int32)


def silu_of_half(half):
    return half * jnp.tanh(half) + half


def normalise(values):
    middle = jnp.mean(values, axis=-1, keepdims=True)
    centred = values - middle
    spread = jnp.mean(centred * centred, axis=-1, keepdims=True)
    return centred * lax.rsqrt(spread + EPSILON)


def placed_rows(ids, numbers):
    block = ids >> 7
    place = jnp.full_like(ids, -1)
    for k, number in enumerate(numbers):
        place = jnp.where(block == number, ids - 128 * (number - k), place)
    return place


def edges_of(ids, sources):
    for e in range(0, 6, GROUP):
        chosen = jnp.concatenate(
            [one_hot(ids[:, k : k + 1], sources.shape[0], 0.5) for k in range(e, e + GROUP)], axis=0
        )
        yield dot(chosen, sources)


def messages(picked_halves, base_of, edge, node, bias_half, gain):
    half_edge = edge * BF16(0.5)
    total = None
    for group, picked in enumerate(picked_halves):
        rows = picked.shape[0] // GROUP
        hidden = jnp.concatenate(
            [
                silu_of_half(picked[k * rows : (k + 1) * rows] + base_of(group * GROUP + k)).astype(BF16)
                for k in range(GROUP)
            ],
            axis=0,
        )
        signals = silu_of_half(dot(hidden, half_edge) + bias_half)
        for k in range(GROUP):
            signal = signals[k * rows : (k + 1) * rows]
            total = signal if total is None else total + signal
    return gain * normalise(dot(total.astype(BF16), node))


def listed_kernel(features, listing, out):
    rows, width = features.shape
    out[pl.ds(0, rows), :] = features[...]
    lists = columns(jnp.broadcast_to(listing[...], (8, listing.shape[1])))[:, :1]
    lists = jnp.broadcast_to(lists.astype(F32), (8, width))
    out[pl.ds(rows, META), :] = jnp.concatenate([lists, jnp.zeros_like(lists)], axis=0).astype(BF16)


def pick(block, number):
    rows = block.shape[0] - META
    listed = block[pl.ds(rows, META), :][number : number + 1, :]
    later = jnp.broadcast_to(listed, (PATCH, block.shape[1])) > BF16(0.5)
    return jnp.where(later, block[pl.ds(PATCH, PATCH), :], block[pl.ds(0, PATCH), :])


def pick_kernel(own, to_next, to_last):
    to_next[...] = pick(own, 4)
    to_last[...] = pick(own, 3)


def bundle_kernel(before, after, to_next, to_last, beside):
    for out, of_after, of_before in ((to_next, 2, 7), (to_last, 0, 5), (beside, 1, 6)):
        out[pl.ds(0, PATCH), :] = pick(after, of_after)
        out[pl.ds(PATCH, PATCH), :] = pick(before, of_before)


def mine_kernel(own, ids, dst, src, bias, own_sources, target_half, src_out, early_place, late_place):
    rows = own_sources.shape[0]
    features = own[pl.ds(0, rows), :]
    own_sources[...] = dot(features, src[...]).astype(BF16)
    target_half[...] = 0.5 * (dot(features, dst[...]) + bias[0:1, :])
    src_out[...] = src[...]
    early_place[...] = columns(placed_rows(ids[...], (0, 1, 3, 8)))
    late_place[...] = columns(placed_rows(ids[...], (5, 6, 2, 7, 4, 9)))


def early_kernel(own_sources, target_half, beside, place, src, base):
    rows = own_sources.shape[0]
    near_sources = dot(beside[...], src[...]).astype(BF16)
    sources = jnp.concatenate([own_sources[...], near_sources], axis=0)
    half = target_half[...]
    for group, picked in enumerate(edges_of(place[...], sources)):
        for k in range(GROUP):
            base[pl.ds((group * GROUP + k) * rows, rows), :] = picked[k * rows : (k + 1) * rows] + half


def fine_kernel(
    own, base, below_own, above_own, below, above, place, cluster, src, edge, node, bias, gain, rows_out, partial_out
):
    rows = rows_out.shape[0]
    pieces = (above_own, below_own, above, below)
    sources = jnp.concatenate([dot(piece[...], src[...]).astype(BF16) for piece in pieces], axis=0)
    update = messages(
        edges_of(place[...], sources),
        lambda e: base[pl.ds(e * rows, rows), :],
        edge[...], node[...], 0.5 * bias[1:2, :], gain[...],
    )
    fine_rows = (own[pl.ds(0, rows), :].astype(F32) + update).astype(BF16)
    rows_out[...] = fine_rows
    clusters = partial_out.shape[0]
    member = lax.broadcasted_iota(jnp.int32, (clusters, rows), 0) == cluster[...]
    member = jnp.where(member, F32(1), F32(0)).astype(BF16)
    partial_out[...] = dot(member, fine_rows).astype(BF16)


def coarse_kernel(spread, fine_rows, ids, cluster, dst, src, edge, node, bias, gain, out, pooled):
    shares = spread.shape[0] // 48
    for k in range(shares):
        pooled[pl.ds(16 * k, 16), :] = spread[pl.ds(48 * k, 16), :]
    clusters = pooled.shape[0]
    sources = dot(spread[...], src[...]).astype(BF16)
    target_half = 0.5 * (dot(pooled[...], dst[...]) + bias[0:1, :])
    place = columns(ids[...])
    within = place & (clusters - 1)
    section = place >> 8
    own = (within >> 4) * 48 + (within & 15)
    side = (within >> 5) * 96 + (within & 31) + 16
    place = jnp.where(section == 1, own, side + (section >> 1) * 48)
    update = messages(
        edges_of(place, sources), lambda e: target_half, edge[...], node[...], 0.5 * bias[1:2, :], gain[...]
    ).astype(BF16)
    owner = columns(jnp.broadcast_to(cluster[...], (8, cluster.shape[1])))[:, :1]
    lifted = dot(one_hot(owner, clusters, 1.0), update)
    out[...] = (fine_rows[...].astype(F32) + lifted).astype(BF16)


def body(
    features,
    neighbours,
    send_list,
    cluster,
    coarse_neighbours,
    fine_dst,
    fine_src,
    fine_edge,
    fine_node,
    fine_bias,
    fine_gain,
    coarse_dst,
    coarse_src,
    coarse_edge,
    coarse_node,
    coarse_bias,
    coarse_gain,
):
    rows, width = features.shape
    shares = lax.axis_size("gather")
    clusters = shares * rows // POOL
    share = clusters // shares
    own = pl.pallas_call(
        listed_kernel,
        out_shape=pltpu.VMEM((rows + META, width), BF16),
        compiler_params=pltpu.CompilerParams(vmem_limit_bytes=8 << 20),
        name="listed",
    )(*far(features, send_list.reshape(1, 8)))
    before = shifted(own, "section", 1)
    after = shifted(own, "section", -1)

    small = pltpu.CompilerParams(vmem_limit_bytes=8 << 20)
    up, down = pl.pallas_call(
        pick_kernel, out_shape=(pltpu.VMEM((PATCH, width), BF16),) * 2, compiler_params=small, name="pick"
    )(*near(own))
    below_own = shifted(up, "gather", 1)
    above_own = shifted(down, "gather", -1)
    to_next, to_last, beside = pl.pallas_call(
        bundle_kernel,
        out_shape=(pltpu.VMEM((2 * PATCH, width), BF16),) * 3,
        compiler_params=small,
        name="bundle",
    )(*near(before, after))
    below = shifted(to_next, "gather", 1)
    above = shifted(to_last, "gather", -1)

    own_sources, target_half, fine_src, early_place, late_place = pl.pallas_call(
        mine_kernel,
        out_shape=(
            pltpu.VMEM((rows, width), BF16),
            pltpu.VMEM((rows, width), F32),
            pltpu.VMEM((width, width), BF16),
            pltpu.VMEM((rows, 6), jnp.int32),
            pltpu.VMEM((rows, 6), jnp.int32),
        ),
        compiler_params=small,
        name="mine",
    )(*near(own), *far(neighbours, fine_dst, fine_src, fine_bias))
    base = pl.pallas_call(
        early_kernel,
        out_shape=pltpu.VMEM((6 * rows, width), F32),
        compiler_params=pltpu.CompilerParams(vmem_limit_bytes=24 << 20),
        name="early",
    )(*near(own_sources, target_half, beside, early_place, fine_src))

    fine_rows, partial = pl.pallas_call(
        fine_kernel,
        out_shape=(
            pltpu.VMEM((rows, width), BF16),
            pltpu.VMEM((clusters, width), BF16),
        ),
        compiler_params=pltpu.CompilerParams(vmem_limit_bytes=24 << 20),
        name="fine",
    )(*near(
        own, base, below_own, above_own, below, above, late_place, cluster[None, :],
        fine_src, fine_edge, fine_node, fine_bias, fine_gain[None, :],
    ))

    parts = lax.all_to_all(partial.reshape(shares, share, width), "gather", 0, 0, tiled=True)
    pooled = (jnp.sum(parts.astype(F32), axis=0) / POOL).astype(BF16)
    side = alternating(across_chip(pooled))
    spread = lax.all_gather(jnp.concatenate([pooled, side], axis=0), "gather", axis=0, tiled=True)

    return pl.pallas_call(
        coarse_kernel,
        out_shape=jax.ShapeDtypeStruct((rows, width), BF16),
        scratch_shapes=[pltpu.VMEM((clusters, width), BF16)],
        compiler_params=pltpu.CompilerParams(vmem_limit_bytes=24 << 20),
        name="coarse",
    )(*near(
        spread, fine_rows, coarse_neighbours, cluster[None, :],
        coarse_dst, coarse_src, coarse_edge, coarse_node, coarse_bias, coarse_gain[None, :],
    ))


def solution(mesh):
    placed = (
        P(("section", "gather"), None),
        P(None, ("section", "gather")),
        P("section", "gather", None, None),
        P(("section", "gather")),
        P(None, "section"),
    ) + (P(),) * 12

    return jax.shard_map(body, mesh=mesh, in_specs=placed, out_specs=P(("section", "gather"), None), check_vma=False)
```
